32 devices in a mesh: rows: 8 (over z, y), ch: 4 (over x, core).
Axes of the slice: x: 2, y: 2, z: 4, core: 2. Of those that a mesh axis runs over, the one named last changes fastest.
Arguments:
- tile_image: bfloat16 [768, 256, 256], P('ch', 'rows'), may hold values from -23 to 23
- spectral_filter: float32 [2, 768, 256, 256], P(None, 'ch', 'rows'), may hold values from -4 to 4
- conv_taps: float32 [768, 9], P('ch'), may hold values from -4 to 4
- norm_gain: float32 [768], replicated, may hold values from 0.25 to 1.75
- up_weight: bfloat16 [768, 3072], P(None, 'ch'), may hold values from -0.21875 to 0.21875
- down_weight: bfloat16 [3072, 768], P('ch'), may hold values from -0.109375 to 0.109375
- upstream: bfloat16 [768, 256, 256], P('ch', 'rows'), may hold values from -5 to 5
Outputs:
- block_out: bfloat16 [768, 256, 256], P('ch', 'rows')
- grad_image: float32 [768, 256, 256], P('ch', 'rows')
- grad_filter: float32 [2, 768, 256, 256], P(None, 'ch', 'rows')
The draws below stay inside these ranges and needn't reach their ends.
All inputs are finite; a program needn't handle non-finite values.
Results may differ from the reference program's by a relative error of at most 0.012.
Values may be sent and summed in bfloat16 or wider, within the bound.
A program may use at most 192 MiB of HBM per device.

```python
import math
import jax
import jax.numpy as jnp
from jax import lax

CHANNEL_COUNT = 768
FF = 3072
H = 256
GRID_COLUMNS = 256
N_CH = 4


def draw_tile_image(key, part):
    entry_key, chan_key, place_key = jax.random.split(key, 3)
    chan_scale = jnp.exp(jax.random.uniform(chan_key, (CHANNEL_COUNT, 1, 1), jnp.float32, math.log(0.3), math.log(3.0)))
    place_scale = jnp.exp(jax.random.uniform(place_key, (1, H, GRID_COLUMNS), jnp.float32, math.log(0.5), math.log(2.0)))
    entries = jax.random.truncated_normal(entry_key, -3.0, 3.0, (CHANNEL_COUNT, H, GRID_COLUMNS), jnp.float32)
    return (entries * chan_scale * place_scale).astype(jnp.bfloat16)


def levels(rng, extent, shards, low, high):
    loudness, own = 1.0, jax.random.fold_in(rng, 6)
    for axis_at, parts in shards:
        heights = jnp.exp(jax.random.uniform(jax.random.fold_in(own, axis_at), (parts,), jnp.float32, low / len(shards), high / len(shards)))
        loudness = loudness * jnp.repeat(heights, extent[axis_at] // parts).reshape([-1 if axis == axis_at else 1 for axis in range(len(extent))])
    return loudness


def normal_values(key, dims, scale, most, cuts=(), held_as=jnp.bfloat16):
    result = scale * jax.random.normal(key, dims, jnp.float32)
    if cuts:
        result = result * levels(key, dims, cuts, -0.22, 0.18)
    return jnp.clip(result, -most, most).astype(held_as)


def setup_inputs(seed: int = 0) -> dict:
    key_list = jax.random.split(jax.random.key(seed), 8)
    return {
        "tile_image": draw_tile_image(jax.random.fold_in(key_list[7], 71), 0),
        "spectral_filter": normal_values(key_list[1], (2, CHANNEL_COUNT, GRID_COLUMNS, H), 0.7, 4.0, ((1, 4), (2, 8)), jnp.float32),
        "conv_taps": normal_values(key_list[2], (CHANNEL_COUNT, 9), 0.33, 4.0, ((0, 4),), jnp.float32),
        "norm_gain": jnp.clip(1.0 + 0.15 * jax.random.normal(key_list[3], (CHANNEL_COUNT,), jnp.float32), 0.25, 1.75),
        "up_weight": normal_values(key_list[4], (CHANNEL_COUNT, FF), CHANNEL_COUNT ** -0.5, 0.21875, ((1, 4),)),
        "down_weight": normal_values(key_list[5], (FF, CHANNEL_COUNT), FF ** -0.5, 0.109375, ((0, 4),)),
        "upstream": normal_values(key_list[6], (CHANNEL_COUNT, H, GRID_COLUMNS), 1.0, 5.0, ((0, 4), (1, 8))),
    }


norm_epsilon = 1e-05
root_half = 0.7071067811865476
density = 0.3989422804014327

def depthwise(values, tap_weights):
    token_row_count, col_count = (values.shape[1], values.shape[2])
    padded = jnp.pad(values, ((0, 0), (1, 1), (1, 1)))
    running = jnp.zeros_like(values)
    for row_off in range(3):
        for col_off in range(3):
            running = running + tap_weights[:, 3 * row_off + col_off][:, None, None] * padded[:, row_off:row_off + token_row_count, col_off:col_off + col_count]
    return running

def layer_norm(whole):
    values = whole.astype(jnp.float32)
    centred = values - lax.optimization_barrier(jnp.mean(values, axis=0))[None]
    inv_std = lax.rsqrt(lax.optimization_barrier(jnp.mean(centred * centred, axis=0)) + norm_epsilon)
    return (centred * inv_std[None], inv_std)

def gelu_slope(pre_act):
    return 0.5 * (1.0 + lax.erf(pre_act * root_half)) + pre_act * density * jnp.exp(-0.5 * pre_act * pre_act)

def norm_back(normed_gradient, normed, inv_std, gain):
    weighted = normed_gradient * gain[None, :, None, None]
    mean_one = lax.optimization_barrier(jnp.mean(weighted, axis=1, keepdims=True))
    second = lax.optimization_barrier(jnp.mean(weighted * normed[None], axis=1, keepdims=True))
    return inv_std[None, None] * (weighted - mean_one - normed[None] * second)

def settle(partials):
    return lax.optimization_barrier(jnp.sum(lax.optimization_barrier(partials.astype(jnp.bfloat16)).astype(jnp.float32), axis=0))

def rounded_copy(values):
    return lax.optimization_barrier(values.astype(jnp.bfloat16)).astype(jnp.float32)

def reference(tile_image, spectral_filter, conv_taps, norm_gain, up_weight, down_weight, upstream):
    signal = tile_image.astype(jnp.float32)
    kernel = jnp.transpose(spectral_filter[0] + 1j * spectral_filter[1], (0, 2, 1))
    spectrum = jnp.fft.fft2(signal, axes=(1, 2))
    filtered = jnp.real(jnp.fft.ifft2(kernel * spectrum, axes=(1, 2)))
    hidden_state = signal + depthwise(filtered, conv_taps)
    complete_up_weight = up_weight.astype(jnp.float32)
    down_full = down_weight.astype(jnp.float32)
    hidden_share_units = FF // N_CH

    def mlp_rows(pieces):
        hidden_rows, grad_rows = pieces
        token_row_count = hidden_rows.shape[1]
        normed, inv_std = layer_norm(lax.optimization_barrier(hidden_rows.astype(jnp.bfloat16)))
        scaled = rounded_copy(normed * norm_gain[:, None, None])
        pre_act = jnp.einsum('chw,cf->fhw', scaled, complete_up_weight)
        activated = rounded_copy(jax.nn.gelu(pre_act, approximate=False))
        partials = jnp.einsum('bfhw,bfc->bchw', activated.reshape(N_CH, hidden_share_units, token_row_count, GRID_COLUMNS), down_full.reshape(N_CH, hidden_share_units, CHANNEL_COUNT))
        out_rows = (hidden_rows + settle(partials)).astype(jnp.bfloat16)
        grad_act = jnp.einsum('chw,fc->fhw', grad_rows.astype(jnp.float32), down_full)
        preactivation_gradient = rounded_copy(grad_act * gelu_slope(pre_act))
        normed_gradient = jnp.einsum('pjra,spj->psra', preactivation_gradient.reshape(N_CH, hidden_share_units, token_row_count, GRID_COLUMNS), complete_up_weight.reshape(CHANNEL_COUNT, N_CH, hidden_share_units))
        return (out_rows, settle(norm_back(normed_gradient, normed, inv_std, norm_gain)))
    block_count = H // 8

    def split_rows(values):
        return jnp.transpose(values.reshape(CHANNEL_COUNT, block_count, 8, GRID_COLUMNS), (1, 0, 2, 3))

    def join_rows(values):
        return jnp.transpose(values, (1, 0, 2, 3)).reshape(CHANNEL_COUNT, H, GRID_COLUMNS)
    out_parts, grad_parts = lax.map(mlp_rows, (split_rows(hidden_state), split_rows(upstream)))
    block_out = join_rows(out_parts)
    grad_hidden = upstream.astype(jnp.float32) + join_rows(grad_parts)
    grad_filtered = depthwise(grad_hidden, conv_taps[:, ::-1])
    grad_spectrum = jnp.fft.fft2(grad_filtered, axes=(1, 2))
    grad_image = grad_hidden + jnp.real(jnp.fft.ifft2(jnp.conj(kernel) * grad_spectrum, axes=(1, 2)))
    factor = 1.0 / (H * GRID_COLUMNS)
    first_part = (grad_spectrum.real * spectrum.real + grad_spectrum.imag * spectrum.imag) * factor
    second_part = (grad_spectrum.imag * spectrum.real - grad_spectrum.real * spectrum.imag) * factor
    grad_filter = jnp.transpose(jnp.stack([first_part, second_part]), (0, 1, 3, 2))
    return (block_out, grad_image, grad_filter)
```

```python
import math

import jax
import jax.numpy as jnp
from jax import lax
from jax.sharding import PartitionSpec as P

norm_epsilon = 1e-05
root_half = 0.7071067811865476
density = 0.3989422804014327


def with_halo(block, sides, width):
    for axis, dim in sides:
        count = lax.axis_size(axis)
        forward = [(i, i + 1) for i in range(count - 1)]
        backward = [(target, source) for source, target in forward]
        low = lax.ppermute(
            lax.slice_in_dim(block, block.shape[dim] - width, None, axis=dim), axis, forward
        )
        high = lax.ppermute(lax.slice_in_dim(block, 0, width, axis=dim), axis, backward)
        block = jnp.concatenate([low, block, high], axis=dim)
    return block


def contract(form, left, right):
    return jnp.einsum(
        form,
        left.astype(jnp.bfloat16),
        right.astype(jnp.bfloat16),
        preferred_element_type=jnp.float32,
    )


def angle_tables(length):
    indices = jnp.arange(length, dtype=jnp.int32)
    products = indices[:, None] * indices[None, :] % length
    angles = products.astype(jnp.float32) * (2.0 * math.pi / length)
    return (jnp.cos(angles), jnp.sin(angles))


def filter_pass(signal, kernel_re, kernel_im):
    col_len = signal.shape[2]
    cos_w, sin_w = angle_tables(col_len)
    head_re = contract("chw,kw->ckh", signal, cos_w)
    head_im = -contract("chw,kw->ckh", signal, sin_w)
    col_re, col_im = (
        lax.all_to_all(
            head_re.astype(jnp.bfloat16), "rows", split_axis=1, concat_axis=2, tiled=True
        ).astype(head_re.dtype),
        lax.all_to_all(
            head_im.astype(jnp.bfloat16), "rows", split_axis=1, concat_axis=2, tiled=True
        ).astype(head_im.dtype),
    )
    row_len = col_re.shape[2]
    cos_h, sin_h = angle_tables(row_len)
    spec_re = contract("cwh,kh->cwk", col_re, cos_h) + contract("cwh,kh->cwk", col_im, sin_h)
    spec_im = contract("cwh,kh->cwk", col_im, cos_h) - contract("cwh,kh->cwk", col_re, sin_h)
    prod_re = kernel_re * spec_re - kernel_im * spec_im
    prod_im = kernel_re * spec_im + kernel_im * spec_re
    back_re = contract("cwk,kh->cwh", prod_re, cos_h) - contract("cwk,kh->cwh", prod_im, sin_h)
    back_im = contract("cwk,kh->cwh", prod_im, cos_h) + contract("cwk,kh->cwh", prod_re, sin_h)
    row_re, row_im = (
        lax.all_to_all(
            back_re.astype(jnp.bfloat16), "rows", split_axis=2, concat_axis=1, tiled=True
        ).astype(back_re.dtype),
        lax.all_to_all(
            back_im.astype(jnp.bfloat16), "rows", split_axis=2, concat_axis=1, tiled=True
        ).astype(back_im.dtype),
    )
    outcome = contract("ckh,kw->chw", row_re, cos_w) - contract("ckh,kw->chw", row_im, sin_w)
    return (outcome * (1.0 / (row_len * col_len)), spec_re, spec_im)


def depthwise(signal, tap_weights):
    token_row_count, col_count = (signal.shape[1], signal.shape[2])
    padded = with_halo(signal.astype(jnp.bfloat16), (("rows", 1),), 1).astype(signal.dtype)
    padded = jnp.pad(padded, ((0, 0), (0, 0), (1, 1)))
    running = jnp.zeros_like(signal)
    for row_off in range(3):
        for col_off in range(3):
            running = (
                running
                + tap_weights[:, 3 * row_off + col_off][:, None, None]
                * padded[:, row_off : row_off + token_row_count, col_off : col_off + col_count]
            )
    return running


def layer_norm(whole):
    values = whole.astype(jnp.float32)
    centred = values - jnp.mean(values, axis=0)[None]
    inv_std = lax.rsqrt(jnp.mean(centred * centred, axis=0) + norm_epsilon)
    return (centred * inv_std[None], inv_std)


def gelu_slope(pre_act):
    return 0.5 * (1.0 + lax.erf(pre_act * root_half)) + pre_act * density * jnp.exp(
        -0.5 * pre_act * pre_act
    )


def norm_back(normed_gradient, normed, inv_std, gain):
    weighted = normed_gradient * gain[None, :, None, None]
    mean_one = jnp.mean(weighted, axis=1, keepdims=True)
    second = jnp.mean(weighted * normed[None], axis=1, keepdims=True)
    return inv_std[None, None] * (weighted - mean_one - normed[None] * second)


def settle(partials):
    return jnp.sum(
        lax.optimization_barrier(partials.astype(jnp.bfloat16)).astype(jnp.float32), axis=0
    )


def to_tokens(values):
    return lax.all_to_all(values, "ch", split_axis=2, concat_axis=0, tiled=True)


def to_channels(values):
    return lax.all_to_all(
        values.astype(jnp.bfloat16), "ch", split_axis=0, concat_axis=2, tiled=True
    ).astype(values.dtype)


def on_device(tile_image, spectral_filter, conv_taps, norm_gain, up_weight, down_weight, upstream):
    signal = tile_image.astype(jnp.float32)
    filtered, spec_re, spec_im = filter_pass(signal, spectral_filter[0], spectral_filter[1])
    hidden_state = signal + depthwise(filtered, conv_taps)
    rounded = hidden_state.astype(jnp.bfloat16)
    gain_column = norm_gain[:, None, None]
    full_up, full_down = (
        lax.all_gather(up_weight, "ch", axis=1, tiled=True),
        lax.all_gather(down_weight, "ch", axis=0, tiled=True),
    )
    blocks = lax.axis_size("ch")
    channels, hidden_units = (full_up.shape[0], full_up.shape[1])
    hidden_share_units = hidden_units // blocks
    normed, inv_std = layer_norm(to_tokens(rounded))
    scaled = (normed * gain_column).astype(jnp.bfloat16)
    pre_act = jnp.einsum("chw,cf->fhw", scaled, full_up, preferred_element_type=jnp.float32)
    activated = jax.nn.gelu(pre_act, approximate=False).astype(jnp.bfloat16)
    token_row_count, col_count = (activated.shape[1], activated.shape[2])
    partials = jnp.einsum(
        "bfhw,bfc->bchw",
        activated.reshape(blocks, hidden_share_units, token_row_count, col_count),
        full_down.reshape(blocks, hidden_share_units, channels),
        preferred_element_type=jnp.float32,
    )
    out_sum = to_channels(settle(partials))
    block_out = (hidden_state + out_sum).astype(jnp.bfloat16)
    whole_dy = to_tokens(upstream)
    grad_act = jnp.einsum("chw,fc->fhw", whole_dy, full_down, preferred_element_type=jnp.float32)
    preactivation_gradient = (grad_act * gelu_slope(pre_act)).astype(jnp.bfloat16)
    normed_gradient = jnp.einsum(
        "pjra,spj->psra",
        preactivation_gradient.reshape(blocks, hidden_share_units, token_row_count, col_count),
        full_up.reshape(channels, blocks, hidden_share_units),
        preferred_element_type=jnp.float32,
    )
    grad_mlp = to_channels(settle(norm_back(normed_gradient, normed, inv_std, norm_gain)))
    grad_hidden = upstream.astype(jnp.float32) + grad_mlp
    grad_filtered = depthwise(grad_hidden, conv_taps[:, ::-1])
    adjoint, grad_re, grad_im = filter_pass(grad_filtered, spectral_filter[0], -spectral_filter[1])
    grad_image = grad_hidden + adjoint
    factor = 1.0 / (tile_image.shape[2] * spec_re.shape[2])
    grad_filter = jnp.stack(
        [
            (grad_re * spec_re + grad_im * spec_im) * factor,
            (grad_im * spec_re - grad_re * spec_im) * factor,
        ]
    )
    return (block_out, grad_image, grad_filter)


def solution(mesh):
    return jax.shard_map(
        on_device,
        mesh=mesh,
        in_specs=(
            P("ch", "rows", None),
            P(None, "ch", "rows", None),
            P("ch", None),
            P(),
            P(None, "ch"),
            P("ch", None),
            P("ch", "rows", None),
        ),
        out_specs=(P("ch", "rows", None), P("ch", "rows", None), P(None, "ch", "rows", None)),
        check_vma=False,
    )
```
